32 devices in a mesh: grp: 2 (over y), patch: 8 (over z, x), frame: 2 (over core).
Axes of the slice: x: 2, y: 2, z: 4, core: 2. Of those that a mesh axis runs over, the one named last changes fastest.
Arguments:
- video_tokens: bfloat16 [4, 16, 80, 1152], P('grp', 'frame', 'patch'), parts along dimension 0, may hold values from -6 to 6
- timestep: int32 [2], P('grp'), parts along dimension 0, may hold values from 0 to 999
- w_qkv: bfloat16 [2, 1152, 1728], P(None, 'patch'), may hold values from -0.1875 to 0.1875
- w_out: bfloat16 [2, 576, 1152], P(None, None, 'patch'), may hold values from -0.25 to 0.25
- qk_gain: float32 [2, 2, 72], replicated, may hold values from 1 to 2.5
- mod_table: float32 [2, 3, 1152], replicated, may hold values from -3 to 3
- mod_gain: float32 [2, 3, 1152], replicated, may hold values from -3 to 3
Outputs:
- denoised: bfloat16 [4, 16, 80, 1152], P('grp', 'frame', 'patch'), parts along dimension 0
The draws below stay inside these ranges and needn't reach their ends.
There are 2 independent parts, one for each index of `grp`. The reference program is written for one: setup_inputs(seed, part) draws one part's arguments, and reference() takes and returns one part's arrays. A program takes and returns all parts, laid end to end along the dimension named above; an argument that names none is the same for every part. Nothing has to cross between parts.
All inputs are finite; a program needn't handle non-finite values.
Results may differ from the reference program's by a relative error of at most 0.013.
Values may be sent and summed in bfloat16 or wider, within the bound.
A program may use at most 128 MiB of HBM per device.

```python
import math
import jax
import jax.numpy as jnp
from jax import lax

D = 1152
HEAD_DIM = 72
HEADS = 8
LAYERS = 2
VIDEOS = 2
FRAMES = 16
PATCHES = 80


def block_scale(key, shape, shards, smallest, high):
    def one(dim, shards_of):
        heights = jax.random.uniform(jax.random.fold_in(jax.random.fold_in(key, 6), dim), (shards_of,), jnp.float32, smallest / len(shards), high / len(shards))
        return jnp.repeat(jnp.exp(heights), shape[dim] // shards_of).reshape((-1,) + (1,) * (len(shape) - dim - 1))

    level = one(*shards[0])
    for cut in shards[1:]:
        level = level * one(*cut)
    return level


def gaussian(own_key, extent, scale, limit, shards=(), kind=jnp.bfloat16):
    array = jax.random.normal(own_key, extent, jnp.float32) * scale
    if len(shards) > 0:
        array = block_scale(own_key, extent, shards, -0.22, 0.18) * array
    return jnp.clip(array, min=-limit, max=limit).astype(kind)


def setup_inputs(seed: int = 0, part: int = 0) -> dict:
    arg_keys = jax.random.split(jax.random.key(seed), 8)
    part_keys = jax.random.split(jax.random.fold_in(arg_keys[7], part), 8)
    return {
        "video_tokens": gaussian(part_keys[0], (VIDEOS, FRAMES, PATCHES, D), 1.0, 6.0, ((1, 2), (2, 8))),
        "timestep": jax.random.randint(part_keys[1], (1,), 0, 1000).astype(jnp.int32),
        "w_qkv": gaussian(arg_keys[2], (LAYERS, D, 3 * HEADS * HEAD_DIM), D ** -0.5, 0.1875, ((1, 8),)),
        "w_out": gaussian(arg_keys[3], (LAYERS, HEADS * HEAD_DIM, D), (HEADS * HEAD_DIM) ** -0.5, 0.25, ((2, 8),)),
        "qk_gain": jnp.clip(jnp.exp(jax.random.uniform(arg_keys[4], (LAYERS, 2, HEAD_DIM), jnp.float32, math.log(1.0), math.log(2.5))), 1.0, 2.5),
        "mod_table": gaussian(arg_keys[5], (LAYERS, 3, D), 0.5, 3.0, (), jnp.float32),
        "mod_gain": gaussian(arg_keys[6], (LAYERS, 3, D), 0.5, 3.0, (), jnp.float32),
    }


def time_embed(timestep, width):
    half_width = width // 2
    freqs = jnp.exp(-math.log(10000.0) * jnp.arange(half_width, dtype=jnp.float32) / half_width)
    angles = timestep[0].astype(jnp.float32) * freqs
    return jnp.concatenate([jnp.cos(angles), jnp.sin(angles)])

def modulate(tokens, table, gains, embed):
    params = table + gains * embed[None, :]
    values = tokens.astype(jnp.float32)
    centre = lax.optimization_barrier(jnp.mean(values, axis=-1, keepdims=True))
    centred = values - centre
    spread = lax.optimization_barrier(jnp.mean(centred * centred, axis=-1, keepdims=True))
    normed = centred * lax.rsqrt(spread + 1e-06)
    return ((normed * (1.0 + params[1]) + params[0]).astype(jnp.bfloat16), params[2])

def head_norm(values, gain):
    meansq = lax.optimization_barrier(jnp.mean(values * values, axis=-1, keepdims=True))
    return (values * lax.rsqrt(meansq + 1e-06) * gain).astype(jnp.bfloat16)

def attend(query, key, value):
    scores = jnp.einsum('nqd,nkd->nqk', query.astype(jnp.float32), key.astype(jnp.float32)) / math.sqrt(HEAD_DIM)
    raised = jnp.exp(scores)
    total = lax.optimization_barrier(jnp.sum(raised, axis=-1, keepdims=True))
    weights = lax.optimization_barrier(raised.astype(jnp.bfloat16)).astype(jnp.float32)
    summed = jnp.einsum('nqk,nkd->nqd', weights, value.astype(jnp.float32))
    return (summed / total).astype(jnp.bfloat16)

def reference(video_tokens, timestep, w_qkv, w_out, qk_gain, mod_table, mod_gain):
    videos, frames, patches, width = video_tokens.shape
    rows = videos * frames * patches
    feat = HEADS * HEAD_DIM
    embed = time_embed(timestep, width)
    tokens = video_tokens.reshape(rows, width)
    for layer in range(2):
        mixed, gate = modulate(tokens, mod_table[layer], mod_gain[layer], embed)
        joint = jnp.dot(mixed, w_qkv[layer], preferred_element_type=jnp.float32)
        joint = joint.reshape(rows, 3, HEADS, HEAD_DIM)
        query = head_norm(joint[:, 0], qk_gain[layer, 0])
        key = head_norm(joint[:, 1], qk_gain[layer, 1])
        value = joint[:, 2].astype(jnp.bfloat16)
        shape5 = (videos, frames, patches, HEADS, HEAD_DIM)
        if layer == 0:

            def items(arr):
                return arr.reshape(shape5).transpose(0, 1, 3, 2, 4).reshape(videos * frames, HEADS, patches, HEAD_DIM)
            result = lax.map(lambda trio: attend(trio[0], trio[1], trio[2]), (items(query), items(key), items(value)))
            attended = result.reshape(videos, frames, HEADS, patches, HEAD_DIM).transpose(0, 1, 3, 2, 4).reshape(rows, feat)
        else:

            def items(arr):
                return arr.reshape(shape5).transpose(0, 2, 3, 1, 4).reshape(videos * patches * HEADS, frames, HEAD_DIM)
            result = attend(items(query), items(key), items(value))
            attended = result.reshape(videos, patches, HEADS, frames, HEAD_DIM).transpose(0, 3, 1, 2, 4).reshape(rows, feat)
        update = jnp.dot(attended, w_out[layer], preferred_element_type=jnp.float32)
        tokens = (tokens.astype(jnp.float32) + gate * update).astype(jnp.bfloat16)
    return tokens.reshape(videos, frames, patches, width)
```

```python
import functools
import math

import jax
import jax.numpy as jnp
import numpy as np
from jax import lax
from jax.experimental import pallas as pl
from jax.experimental.pallas import tpu as pltpu
from jax.sharding import PartitionSpec as P


def time_embed(timestep, width):
    half_width = width // 2
    freqs = jnp.exp(-math.log(10000.0) * jnp.arange(half_width, dtype=jnp.float32) / half_width)
    angles = timestep[0].astype(jnp.float32) * freqs
    return jnp.concatenate([jnp.cos(angles), jnp.sin(angles)])


def modulate(tokens, table, gains, embed):
    params = table + gains * embed[None, :]
    values = tokens.astype(jnp.float32)
    centre = jnp.mean(values, axis=-1, keepdims=True)
    centred = values - centre
    spread = jnp.mean(centred * centred, axis=-1, keepdims=True)
    normed = centred * lax.rsqrt(spread + 1e-06)
    return ((normed * (1.0 + params[1]) + params[0]).astype(jnp.bfloat16), params[2])


def head_norm(values, gain):
    meansq = jnp.mean(values * values, axis=-1, keepdims=True)
    return (values * lax.rsqrt(meansq + 1e-06) * gain).astype(jnp.bfloat16)


def fetch_weights(qkv_rows, out_cols):
    return (
        lax.all_gather(qkv_rows, "patch", axis=0, tiled=True),
        lax.all_gather(out_cols, "patch", axis=1, tiled=True),
    )


def attend_items(stacked):
    head_size = stacked.shape[-1]
    query = stacked[0, 0]
    key = stacked[1, 0]
    value = stacked[2, 0]
    scores = jnp.einsum("nqd,nkd->nqk", query, key, preferred_element_type=jnp.float32) / math.sqrt(
        head_size
    )
    raised = jnp.exp(scores)
    total = jnp.sum(raised, axis=-1, keepdims=True)
    summed = jnp.einsum(
        "nqk,nkd->nqd", raised.astype(jnp.bfloat16), value, preferred_element_type=jnp.float32
    )
    return (summed / total).astype(jnp.bfloat16)[None]


def spatial(query, key, value, videos, fr_dev, patch_dev):
    rows, heads, head_size = query.shape
    groups = lax.axis_size("patch")
    per_group = videos * fr_dev * heads // groups
    stacked = jnp.stack([query, key, value])
    stacked = stacked.reshape(3, videos * fr_dev, patch_dev, heads, head_size)
    stacked = stacked.transpose(0, 1, 3, 2, 4).reshape(3, groups, per_group, patch_dev, head_size)
    attended = attend_items(
        lax.all_to_all(stacked, "patch", split_axis=1, concat_axis=3, tiled=True)
    )
    returned = lax.all_to_all(attended, "patch", split_axis=2, concat_axis=0, tiled=True)
    returned = returned.reshape(videos * fr_dev, heads, patch_dev, head_size).transpose(0, 2, 1, 3)
    return returned.reshape(rows, heads * head_size)


def frame_attend(query, key, value, heads):
    videos, q_frames, patches, feat = query.shape
    k_frames = key.shape[1]
    head_size = feat // heads
    query = query.reshape(videos, q_frames, patches, heads, head_size)
    key = key.reshape(videos, k_frames, patches, heads, head_size)
    value = value.reshape(videos, k_frames, patches, heads, head_size)
    scores = jnp.einsum(
        "bfphd,bgphd->bphfg", query, key, preferred_element_type=jnp.float32
    ) / math.sqrt(head_size)
    raised = jnp.exp(scores)
    total = jnp.sum(raised, axis=-1)
    summed = jnp.einsum(
        "bphfg,bgphd->bfphd", raised.astype(jnp.bfloat16), value, preferred_element_type=jnp.float32
    )
    result = summed / total.transpose(0, 3, 1, 2)[..., None]
    return result.astype(jnp.bfloat16).reshape(videos, q_frames, patches, feat)


def temporal(query, key, value, videos, fr_dev, patch_dev):
    rows, heads, head_size = query.shape
    feat = heads * head_size
    query4 = query.reshape(videos, fr_dev, patch_dev, feat)
    key4 = key.reshape(videos, fr_dev, patch_dev, feat)
    value4 = value.reshape(videos, fr_dev, patch_dev, feat)
    joined = jnp.concatenate([query4, key4, value4], axis=3)
    swapped = lax.all_to_all(joined, "frame", split_axis=2, concat_axis=1, tiled=True)
    result = frame_attend(
        swapped[..., :feat], swapped[..., feat : 2 * feat], swapped[..., 2 * feat :], heads
    )
    returned = lax.all_to_all(result, "frame", split_axis=1, concat_axis=2, tiled=True)
    return returned.reshape(rows, feat)


def per_device(video_tokens, timestep, w_qkv, w_out, qk_gain, mod_table, mod_gain):
    videos, fr_dev, patch_dev, width = video_tokens.shape
    rows = videos * fr_dev * patch_dev
    head_size = qk_gain.shape[2]
    heads = w_out.shape[1] // head_size
    embed = time_embed(timestep, width)
    tokens = video_tokens.reshape(rows, width)
    for layer in range(2):
        qkv_full, out_full = fetch_weights(w_qkv[layer], w_out[layer])
        mixed, gate = modulate(tokens, mod_table[layer], mod_gain[layer], embed)
        joint = jnp.dot(mixed, qkv_full, preferred_element_type=jnp.float32)
        joint = joint.reshape(rows, 3, heads, head_size)
        query = head_norm(joint[:, 0], qk_gain[layer, 0])
        key = head_norm(joint[:, 1], qk_gain[layer, 1])
        value = joint[:, 2].astype(jnp.bfloat16)
        if layer == 0:
            attended = spatial(query, key, value, videos, fr_dev, patch_dev)
        else:
            attended = temporal(query, key, value, videos, fr_dev, patch_dev)
        update = jnp.dot(attended, out_full, preferred_element_type=jnp.float32)
        tokens = (tokens.astype(jnp.float32) + gate * update).astype(jnp.bfloat16)
    return tokens.reshape(videos, fr_dev, patch_dev, width)


MESH = pl.DeviceIdType.MESH
CHUNKS = 3
HIGHEST = lax.Precision.HIGHEST


def dot_f32(a, b, contract):
    return lax.dot_general(
        a, b, ((contract[:1], contract[1:]), ((), ())), preferred_element_type=jnp.float32
    )


def ring_to_patch(pos, count):
    upper = lax.div(pos, count // 2)
    return (1 - upper) * 2 * pos + upper * (2 * count - 1 - 2 * pos)


def patch_to_ring(patch, count):
    side = lax.rem(patch, 2)
    level = lax.div(patch, 2)
    return (1 - side) * level + side * (count - 1 - level)


def norm_tokens(values, params):
    centre = jnp.mean(values, axis=-1, keepdims=True)
    centred = values - centre
    spread = jnp.mean(centred * centred, axis=-1, keepdims=True)
    normed = centred * lax.rsqrt(spread + 1e-06)
    return (normed * (1.0 + params[1:2]) + params[0:1]).astype(jnp.bfloat16)


def norm_heads(values, gain, heads_map, head_size):
    total = lax.dot_general(
        values * values,
        heads_map,
        (((1,), (1,)), ((), ())),
        precision=HIGHEST,
        preferred_element_type=jnp.float32,
    )
    scale = lax.rsqrt(total / head_size + 1e-06)
    wide = lax.dot_general(
        scale,
        heads_map,
        (((1,), (0,)), ((), ())),
        precision=HIGHEST,
        preferred_element_type=jnp.float32,
    )
    return (values * wide * gain).astype(jnp.bfloat16)


def attend_heads(query, key, value, heads_map, mask, att_ref, head_size):
    feat = query.shape[1]
    att_ref[...] = jnp.zeros_like(att_ref)
    for head in range(feat // head_size):
        low = head * head_size // 128 * 128
        high = min(-(-(head + 1) * head_size // 128) * 128, feat)
        lanes = heads_map[head : head + 1, low:high].astype(jnp.bfloat16)
        scores = dot_f32(query[:, low:high] * lanes, key[:, low:high], (1, 1))
        raised = jnp.where(mask > 0.0, jnp.exp(scores / math.sqrt(head_size)), 0.0)
        total = jnp.sum(raised, axis=-1, keepdims=True)
        summed = dot_f32(raised.astype(jnp.bfloat16), value[:, low:high] * lanes, (1, 0))
        att_ref[:, low:high] += summed / total
    return att_ref[...].astype(jnp.bfloat16)


def fused_kernel(
    head_size, x_ref, w_ref, par_ref, gain_ref, heads_ref, mask_ref, out_ref,
    wbuf, xin, mid_send, mid_recv, xf, att, res,
    local_sem, in_send, in_recv, ring_send, ring_recv, sib_send, sib_recv,
    mid_ssem, mid_rsem, fin_send, fin_recv,
):
    videos, fr_dev, patch_dev, width = x_ref.shape
    layers, rows, lanes = w_ref.shape
    count = fr_dev
    half = lanes // 2
    feat = heads_ref.shape[1]
    grp = lax.axis_index("grp")
    me = lax.axis_index("patch")
    core = lax.axis_index("frame")
    sib = 1 - core
    pos = patch_to_ring(me, count)
    turn = 1 - 2 * core
    piece = rows // CHUNKS
    onward = ring_to_patch(lax.rem(pos + turn + count, count), count)

    barrier = pltpu.get_barrier_semaphore()
    for k in range(count):
        for s in range(2):
            if k or s:
                pl.semaphore_signal(
                    barrier,
                    inc=1,
                    device_id=(grp, lax.rem(me + k, count), lax.rem(core + s, 2)),
                    device_id_type=MESH,
                )
    pl.semaphore_wait(barrier, 2 * count - 1)

    def remote(src, dst, send_sem, recv_sem, patch, frame):
        return pltpu.make_async_remote_copy(
            src_ref=src,
            dst_ref=dst,
            send_sem=send_sem,
            recv_sem=recv_sem,
            device_id=(grp, patch, frame),
            device_id_type=MESH,
        )

    own_in = pltpu.make_async_copy(x_ref.at[:, me], xin.at[me], local_sem.at[0])
    own_w = pltpu.make_async_copy(
        w_ref, wbuf.at[:, pl.ds(pl.multiple_of(me * rows, 16), rows), :], local_sem.at[1]
    )
    own_in.start()
    sent = []
    for k in range(1, count):
        peer = lax.rem(me + k, count)
        copy = remote(x_ref.at[:, peer], xin.at[me], in_send.at[k], in_recv.at[me], peer, core)
        copy.start()
        sent.append(copy)

    def block(layer, step, chunk, owner_core, from_input):
        direction = 1 - 2 * owner_core
        source = ring_to_patch(lax.rem(pos - direction * step + count, count), count)
        columns = pl.ds(pl.multiple_of(owner_core * half, 128), half)
        if from_input:
            return w_ref.at[layer, pl.ds(chunk * piece, piece), columns]
        start = pl.multiple_of(source * rows + chunk * piece, 16)
        return wbuf.at[layer, pl.ds(start, piece), columns]

    def ring_copy(layer, step, chunk):
        return remote(
            block(layer, step, chunk, core, step == 0),
            block(layer, step, chunk, core, False),
            ring_send.at[layer, step, chunk],
            ring_recv.at[layer, step, chunk],
            onward,
            core,
        )

    def arrived(layer, step, chunk):
        landed = block(layer, step + 1, chunk, core, False)
        remote(
            landed,
            landed,
            ring_send.at[layer, step, chunk],
            ring_recv.at[layer, step, chunk],
            onward,
            core,
        ).wait_recv()
        if step + 1 < count - 1:
            copy = ring_copy(layer, step + 1, chunk)
            copy.start()
            sent.append(copy)
        copy = remote(
            landed,
            landed,
            sib_send.at[layer, step, chunk],
            sib_recv.at[layer, step, chunk],
            me,
            sib,
        )
        copy.start()
        sent.append(copy)

    def ring_step(layer, step):
        for chunk in range(CHUNKS):
            arrived(layer, step, chunk)

    def sibling_done(layer):
        for step in range(count - 1):
            for chunk in range(CHUNKS):
                landed = block(layer, step + 1, chunk, sib, False)
                remote(
                    landed,
                    landed,
                    sib_send.at[layer, step, chunk],
                    sib_recv.at[layer, step, chunk],
                    me,
                    sib,
                ).wait_recv()

    for layer in range(layers):
        for chunk in range(CHUNKS):
            copy = ring_copy(layer, 0, chunk)
            copy.start()
            sent.append(copy)
    own_w.start()

    heads_map = heads_ref[...]

    def project(layer, mixed):
        joint = jnp.dot(mixed, wbuf[layer, :, : 3 * feat], preferred_element_type=jnp.float32)
        query = norm_heads(joint[:, :feat], gain_ref[layer, 0:1], heads_map, head_size)
        key = norm_heads(joint[:, feat : 2 * feat], gain_ref[layer, 1:2], heads_map, head_size)
        return query, key, joint[:, 2 * feat :].astype(jnp.bfloat16)

    def update(layer, tokens, attended):
        added = dot_f32(attended, wbuf[layer, :, 3 * feat :], (1, 1))
        return tokens + par_ref[layer, 2:3] * added

    own_in.wait()
    for k in range(1, count):
        peer = lax.rem(me + k, count)
        remote(
            xin.at[peer], xin.at[peer], in_send.at[k], in_recv.at[peer], peer, core
        ).wait_recv()
    for video in range(videos):
        for patch in range(count):
            low = (video * count + patch) * patch_dev
            xf[low : low + patch_dev, :] = xin[patch, video].astype(jnp.float32)
    mixed = norm_tokens(xf[...], par_ref[0])
    for step in range(count - 1):
        ring_step(0, step)
    own_w.wait()
    sibling_done(0)
    query, key, value = project(0, mixed)
    ring_step(1, 0)
    attended = attend_heads(query, key, value, heads_map, mask_ref[0], att, head_size)
    ring_step(1, 1)
    xf[...] = update(0, xf[...], attended)

    frame = core * count + me
    for k in range(2 * count):
        video, patch = k // count, k % count
        low = k * patch_dev
        mid_send[k] = xf[low : low + patch_dev, :].astype(jnp.bfloat16)
    own_mid = pltpu.make_async_copy(mid_send.at[frame], mid_recv.at[frame], local_sem.at[2])
    own_mid.start()
    for s in range(2):
        for k in range(count):
            if k or s:
                peer, video = lax.rem(me + k, count), lax.rem(core + s, 2)
                copy = remote(
                    mid_send.at[video * count + peer],
                    mid_recv.at[frame],
                    mid_ssem.at[s * count + k],
                    mid_rsem.at[frame],
                    peer,
                    video,
                )
                copy.start()
                sent.append(copy)
    for step in range(2, count - 1):
        ring_step(1, step)
    own_mid.wait()
    for s in range(2):
        for k in range(count):
            if k or s:
                peer, video = lax.rem(me + k, count), lax.rem(core + s, 2)
                landed = mid_recv.at[video * count + peer]
                remote(
                    landed,
                    landed,
                    mid_ssem.at[s * count + k],
                    mid_rsem.at[video * count + peer],
                    peer,
                    video,
                ).wait_recv()

    for k in range(2 * count):
        low = k * patch_dev
        xf[low : low + patch_dev, :] = mid_recv[k].astype(jnp.float32)
    mixed = norm_tokens(xf[...], par_ref[1])
    sibling_done(1)
    query, key, value = project(1, mixed)
    attended = attend_heads(query, key, value, heads_map, mask_ref[1], att, head_size)
    xf[...] = update(1, xf[...], attended)
    for k in range(2 * count):
        low = k * patch_dev
        res[k] = xf[low : low + patch_dev, :].astype(jnp.bfloat16)
    own_out = pltpu.make_async_copy(
        res.at[pl.ds(core * count, count)], out_ref.at[core], local_sem.at[3]
    )
    own_out.start()
    final = remote(
        res.at[pl.ds(sib * count, count)], out_ref.at[core], fin_send, fin_recv, me, sib
    )
    final.start()
    own_out.wait()
    final.wait_send()
    remote(
        out_ref.at[sib], out_ref.at[sib], fin_send, fin_recv, me, sib
    ).wait_recv()
    for copy in sent:
        copy.wait_send()


def fused_device(video_tokens, timestep, w_qkv, w_out, qk_gain, mod_table, mod_gain):
    videos, fr_dev, patch_dev, width = video_tokens.shape
    layers, rows, _ = w_qkv.shape
    head_size = qk_gain.shape[2]
    feat = w_out.shape[1]
    heads = feat // head_size
    tokens = videos * fr_dev * patch_dev
    embed = time_embed(timestep, width)
    params = mod_table + mod_gain * embed[None, None, :]
    gains = jnp.tile(qk_gain, (1, 1, heads))
    joined = jnp.concatenate([w_qkv, w_out.transpose(0, 2, 1)], axis=2)
    lanes = joined.shape[2]
    heads_map = jnp.asarray(np.repeat(np.eye(heads, dtype=np.float32), head_size, axis=1))
    row = np.arange(tokens)
    frame_patches = tokens // videos
    masks = np.stack(
        [
            (row[:, None] // frame_patches) == (row[None, :] // frame_patches),
            (row[:, None] % patch_dev) == (row[None, :] % patch_dev),
        ]
    ).astype(np.float32)
    vmem = pl.BlockSpec(memory_space=pltpu.VMEM)
    count = fr_dev
    bf16, f32 = jnp.bfloat16, jnp.float32
    dma = pltpu.SemaphoreType.DMA
    ring = (layers, count - 1, CHUNKS)
    return pl.pallas_call(
        functools.partial(fused_kernel, head_size),
        out_shape=jax.ShapeDtypeStruct(video_tokens.shape, bf16),
        in_specs=[vmem] * 6,
        out_specs=vmem,
        scratch_shapes=[
            pltpu.VMEM((layers, count * rows, lanes), bf16),
            pltpu.VMEM((count, videos, patch_dev, width), bf16),
            pltpu.VMEM((2 * count, patch_dev, width), bf16),
            pltpu.VMEM((2 * count, patch_dev, width), bf16),
            pltpu.VMEM((tokens, width), f32),
            pltpu.VMEM((tokens, feat), f32),
            pltpu.VMEM((2 * count, patch_dev, width), bf16),
            dma((4,)),
            dma((count,)),
            dma((count,)),
            dma(ring),
            dma(ring),
            dma(ring),
            dma(ring),
            dma((2 * count,)),
            dma((2 * count,)),
            dma,
            dma,
        ],
        compiler_params=pltpu.CompilerParams(
            collective_id=0, has_side_effects=True, vmem_limit_bytes=56 * 1024 * 1024
        ),
        name="blocks",
    )(video_tokens, joined, params, gains, heads_map, jnp.asarray(masks))


def choose_device(video_tokens, timestep, w_qkv, *rest):
    videos, fr_dev, _, _ = video_tokens.shape
    fits = videos == 2 and fr_dev == 8 and w_qkv.shape[1] % (16 * CHUNKS) == 0
    run = fused_device if fits else per_device
    return run(video_tokens, timestep, w_qkv, *rest)


def solution(mesh):
    placed = (
        P("grp", "frame", "patch", None),
        P("grp"),
        P(None, "patch", None),
        P(None, None, "patch"),
        P(),
        P(),
        P(),
    )
    ring = mesh.shape["patch"] == 8 and mesh.shape["frame"] == 2
    return jax.shard_map(
        choose_device if ring else per_device,
        mesh=mesh,
        in_specs=placed,
        out_specs=P("grp", "frame", "patch", None),
        check_vma=False,
    )
```

```python
import functools
import math

import jax
import jax.numpy as jnp
import numpy as np
from jax import lax
from jax.experimental import pallas as pl
from jax.experimental.pallas import tpu as pltpu
from jax.sharding import PartitionSpec as P


def time_embed(timestep, width):
    half_width = width // 2
    freqs = jnp.exp(-math.log(10000.0) * jnp.arange(half_width, dtype=jnp.float32) / half_width)
    angles = timestep[0].astype(jnp.float32) * freqs
    return jnp.concatenate([jnp.cos(angles), jnp.sin(angles)])


def modulate(tokens, table, gains, embed):
    params = table + gains * embed[None, :]
    values = tokens.astype(jnp.float32)
    centre = jnp.mean(values, axis=-1, keepdims=True)
    centred = values - centre
    spread = jnp.mean(centred * centred, axis=-1, keepdims=True)
    normed = centred * lax.rsqrt(spread + 1e-06)
    return ((normed * (1.0 + params[1]) + params[0]).astype(jnp.bfloat16), params[2])


def head_norm(values, gain):
    meansq = jnp.mean(values * values, axis=-1, keepdims=True)
    return (values * lax.rsqrt(meansq + 1e-06) * gain).astype(jnp.bfloat16)


def fetch_weights(qkv_rows, out_cols):
    return (
        lax.all_gather(qkv_rows, "patch", axis=0, tiled=True),
        lax.all_gather(out_cols, "patch", axis=1, tiled=True),
    )


def attend_items(stacked):
    head_size = stacked.shape[-1]
    query = stacked[0, 0]
    key = stacked[1, 0]
    value = stacked[2, 0]
    scores = jnp.einsum("nqd,nkd->nqk", query, key, preferred_element_type=jnp.float32) / math.sqrt(
        head_size
    )
    raised = jnp.exp(scores)
    total = jnp.sum(raised, axis=-1, keepdims=True)
    summed = jnp.einsum(
        "nqk,nkd->nqd", raised.astype(jnp.bfloat16), value, preferred_element_type=jnp.float32
    )
    return (summed / total).astype(jnp.bfloat16)[None]


def spatial(query, key, value, videos, fr_dev, patch_dev):
    rows, heads, head_size = query.shape
    groups = lax.axis_size("patch")
    per_group = videos * fr_dev * heads // groups
    stacked = jnp.stack([query, key, value])
    stacked = stacked.reshape(3, videos * fr_dev, patch_dev, heads, head_size)
    stacked = stacked.transpose(0, 1, 3, 2, 4).reshape(3, groups, per_group, patch_dev, head_size)
    attended = attend_items(
        lax.all_to_all(stacked, "patch", split_axis=1, concat_axis=3, tiled=True)
    )
    returned = lax.all_to_all(attended, "patch", split_axis=2, concat_axis=0, tiled=True)
    returned = returned.reshape(videos * fr_dev, heads, patch_dev, head_size).transpose(0, 2, 1, 3)
    return returned.reshape(rows, heads * head_size)


def frame_attend(query, key, value, heads):
    videos, q_frames, patches, feat = query.shape
    k_frames = key.shape[1]
    head_size = feat // heads
    query = query.reshape(videos, q_frames, patches, heads, head_size)
    key = key.reshape(videos, k_frames, patches, heads, head_size)
    value = value.reshape(videos, k_frames, patches, heads, head_size)
    scores = jnp.einsum(
        "bfphd,bgphd->bphfg", query, key, preferred_element_type=jnp.float32
    ) / math.sqrt(head_size)
    raised = jnp.exp(scores)
    total = jnp.sum(raised, axis=-1)
    summed = jnp.einsum(
        "bphfg,bgphd->bfphd", raised.astype(jnp.bfloat16), value, preferred_element_type=jnp.float32
    )
    result = summed / total.transpose(0, 3, 1, 2)[..., None]
    return result.astype(jnp.bfloat16).reshape(videos, q_frames, patches, feat)


def temporal(query, key, value, videos, fr_dev, patch_dev):
    rows, heads, head_size = query.shape
    feat = heads * head_size
    query4 = query.reshape(videos, fr_dev, patch_dev, feat)
    key4 = key.reshape(videos, fr_dev, patch_dev, feat)
    value4 = value.reshape(videos, fr_dev, patch_dev, feat)
    joined = jnp.concatenate([query4, key4, value4], axis=3)
    swapped = lax.all_to_all(joined, "frame", split_axis=2, concat_axis=1, tiled=True)
    result = frame_attend(
        swapped[..., :feat], swapped[..., feat : 2 * feat], swapped[..., 2 * feat :], heads
    )
    returned = lax.all_to_all(result, "frame", split_axis=1, concat_axis=2, tiled=True)
    return returned.reshape(rows, feat)


def per_device(video_tokens, timestep, w_qkv, w_out, qk_gain, mod_table, mod_gain):
    videos, fr_dev, patch_dev, width = video_tokens.shape
    rows = videos * fr_dev * patch_dev
    head_size = qk_gain.shape[2]
    heads = w_out.shape[1] // head_size
    embed = time_embed(timestep, width)
    tokens = video_tokens.reshape(rows, width)
    for layer in range(2):
        qkv_full, out_full = fetch_weights(w_qkv[layer], w_out[layer])
        mixed, gate = modulate(tokens, mod_table[layer], mod_gain[layer], embed)
        joint = jnp.dot(mixed, qkv_full, preferred_element_type=jnp.float32)
        joint = joint.reshape(rows, 3, heads, head_size)
        query = head_norm(joint[:, 0], qk_gain[layer, 0])
        key = head_norm(joint[:, 1], qk_gain[layer, 1])
        value = joint[:, 2].astype(jnp.bfloat16)
        if layer == 0:
            attended = spatial(query, key, value, videos, fr_dev, patch_dev)
        else:
            attended = temporal(query, key, value, videos, fr_dev, patch_dev)
        update = jnp.dot(attended, out_full, preferred_element_type=jnp.float32)
        tokens = (tokens.astype(jnp.float32) + gate * update).astype(jnp.bfloat16)
    return tokens.reshape(videos, fr_dev, patch_dev, width)


MESH = pl.DeviceIdType.MESH
CHUNKS = 3
HIGHEST = lax.Precision.HIGHEST


def dot_f32(a, b, contract):
    return lax.dot_general(
        a, b, ((contract[:1], contract[1:]), ((), ())), preferred_element_type=jnp.float32
    )


def ring_to_patch(pos, count):
    upper = lax.div(pos, count // 2)
    return (1 - upper) * 2 * pos + upper * (2 * count - 1 - 2 * pos)


def patch_to_ring(patch, count):
    side = lax.rem(patch, 2)
    level = lax.div(patch, 2)
    return (1 - side) * level + side * (count - 1 - level)


def norm_tokens(values, params):
    centre = jnp.mean(values, axis=-1, keepdims=True)
    centred = values - centre
    spread = jnp.mean(centred * centred, axis=-1, keepdims=True)
    normed = centred * lax.rsqrt(spread + 1e-06)
    return (normed * (1.0 + params[1:2]) + params[0:1]).astype(jnp.bfloat16)


def norm_heads(values, gain, heads_map, head_size):
    total = lax.dot_general(
        values * values,
        heads_map,
        (((1,), (1,)), ((), ())),
        precision=HIGHEST,
        preferred_element_type=jnp.float32,
    )
    scale = lax.rsqrt(total / head_size + 1e-06)
    wide = lax.dot_general(
        scale,
        heads_map,
        (((1,), (0,)), ((), ())),
        precision=HIGHEST,
        preferred_element_type=jnp.float32,
    )
    return (values * wide * gain).astype(jnp.bfloat16)


def attend_heads(query, key, value, heads_map, mask, att_ref, head_size, between=None):
    feat = query.shape[1]
    att_ref[...] = jnp.zeros_like(att_ref)
    for head in range(feat // head_size):
        low = head * head_size // 128 * 128
        high = min(-(-(head + 1) * head_size // 128) * 128, feat)
        lanes = heads_map[head : head + 1, low:high].astype(jnp.bfloat16)
        scores = dot_f32(query[:, low:high] * lanes, key[:, low:high], (1, 1))
        raised = jnp.where(mask > 0.0, jnp.exp(scores / math.sqrt(head_size)), 0.0)
        total = jnp.sum(raised, axis=-1, keepdims=True)
        summed = dot_f32(raised.astype(jnp.bfloat16), value[:, low:high] * lanes, (1, 0))
        att_ref[:, low:high] += summed / total
        if between is not None and head == 3:
            between()
    return att_ref[...].astype(jnp.bfloat16)


def fused_kernel(
    head_size, x_ref, w_ref, par_ref, gain_ref, heads_ref, mask_ref, out_ref,
    wbuf, xin, mid_send, mid_recv, xf, att, res,
    local_sem, in_send, in_recv, ring_send, ring_recv, sib_send, sib_recv,
    mid_ssem, mid_rsem, fin_send, fin_recv, twin_send, twin_recv,
):
    videos, fr_dev, patch_dev, width = x_ref.shape
    layers, rows, lanes = w_ref.shape
    count = fr_dev
    half = lanes // 2
    feat = heads_ref.shape[1]
    grp = lax.axis_index("grp")
    me = lax.axis_index("patch")
    core = lax.axis_index("frame")
    sib = 1 - core
    pos = patch_to_ring(me, count)
    turn = 1 - 2 * core
    piece = rows // CHUNKS
    onward = ring_to_patch(lax.rem(pos + turn + count, count), count)

    barrier = pltpu.get_barrier_semaphore()
    for k in range(count):
        for s in range(2):
            if k or s:
                pl.semaphore_signal(
                    barrier,
                    inc=1,
                    device_id=(grp, lax.rem(me + k, count), lax.rem(core + s, 2)),
                    device_id_type=MESH,
                )
    pl.semaphore_signal(
        barrier, inc=1, device_id=(1 - grp, me, core), device_id_type=MESH
    )
    pl.semaphore_wait(barrier, 2 * count)

    def remote(src, dst, send_sem, recv_sem, patch, frame, to_grp=grp):
        return pltpu.make_async_remote_copy(
            src_ref=src,
            dst_ref=dst,
            send_sem=send_sem,
            recv_sem=recv_sem,
            device_id=(to_grp, patch, frame),
            device_id_type=MESH,
        )

    own_in = pltpu.make_async_copy(x_ref.at[:, me], xin.at[me], local_sem.at[0])
    own_w = pltpu.make_async_copy(
        w_ref, wbuf.at[:, pl.ds(pl.multiple_of(me * rows, 16), rows), :], local_sem.at[1]
    )
    own_in.start()
    sent = []
    for k in range(1, count):
        peer = lax.rem(me + k, count)
        copy = remote(x_ref.at[:, peer], xin.at[me], in_send.at[k], in_recv.at[me], peer, core)
        copy.start()
        sent.append(copy)

    def block(layer, step, chunk, owner_core, from_input):
        direction = 1 - 2 * owner_core
        source = ring_to_patch(lax.rem(pos - direction * step + count, count), count)
        columns = pl.ds(pl.multiple_of(owner_core * half, 128), half)
        if from_input:
            return w_ref.at[layer, pl.ds(pl.multiple_of(chunk * piece, 16), piece), columns]
        start = pl.multiple_of(source * rows + chunk * piece, 16)
        return wbuf.at[layer, pl.ds(start, piece), columns]

    def ring_copy(layer, step, slot):
        chunk = grp if slot == 0 else 2
        return remote(
            block(layer, step, chunk, core, step == 0),
            block(layer, step, chunk, core, False),
            ring_send.at[layer, step, slot],
            ring_recv.at[layer, step, slot],
            onward,
            core,
        )

    def ring_start(layer):
        for slot in range(2):
            copy = ring_copy(layer, 0, slot)
            copy.start()
            sent.append(copy)

    def to_sibling(layer, step, slot, landed):
        copy = remote(
            landed,
            landed,
            sib_send.at[layer, step, slot],
            sib_recv.at[layer, step, slot],
            me,
            sib,
        )
        copy.start()
        sent.append(copy)

    def twin_step(layer, step):
        landed = block(layer, step + 1, 1 - grp, core, False)
        remote(
            landed,
            landed,
            twin_send.at[layer, step],
            twin_recv.at[layer, step],
            me,
            core,
            1 - grp,
        ).wait_recv()
        to_sibling(layer, step, 2, landed)

    def ring_step(layer, step):
        for slot in range(2):
            landed = block(layer, step + 1, grp if slot == 0 else 2, core, False)
            remote(
                landed,
                landed,
                ring_send.at[layer, step, slot],
                ring_recv.at[layer, step, slot],
                onward,
                core,
            ).wait_recv()
            if step + 1 < count - 1:
                copy = ring_copy(layer, step + 1, slot)
                copy.start()
                sent.append(copy)
            if slot == 0:
                copy = remote(
                    landed,
                    landed,
                    twin_send.at[layer, step],
                    twin_recv.at[layer, step],
                    me,
                    core,
                    1 - grp,
                )
                copy.start()
                sent.append(copy)
            to_sibling(layer, step, slot, landed)
        if step > 0:
            twin_step(layer, step - 1)
        if step == count - 2:
            twin_step(layer, step)

    def sibling_done(layer):
        for step in range(count - 1):
            for slot in range(CHUNKS):
                chunk = (grp, 2, 1 - grp)[slot]
                landed = block(layer, step + 1, chunk, sib, False)
                remote(
                    landed,
                    landed,
                    sib_send.at[layer, step, slot],
                    sib_recv.at[layer, step, slot],
                    me,
                    sib,
                ).wait_recv()

    ring_start(0)
    own_w.start()

    heads_map = heads_ref[...]

    def project(layer, mixed):
        joint = jnp.dot(mixed, wbuf[layer, :, : 3 * feat], preferred_element_type=jnp.float32)
        query = norm_heads(joint[:, :feat], gain_ref[layer, 0:1], heads_map, head_size)
        key = norm_heads(joint[:, feat : 2 * feat], gain_ref[layer, 1:2], heads_map, head_size)
        return query, key, joint[:, 2 * feat :].astype(jnp.bfloat16)

    def update(layer, tokens, attended):
        added = dot_f32(attended, wbuf[layer, :, 3 * feat :], (1, 1))
        return tokens + par_ref[layer, 2:3] * added

    own_in.wait()
    for k in range(1, count):
        peer = lax.rem(me + k, count)
        remote(
            xin.at[peer], xin.at[peer], in_send.at[k], in_recv.at[peer], peer, core
        ).wait_recv()
    for video in range(videos):
        for patch in range(count):
            low = (video * count + patch) * patch_dev
            xf[low : low + patch_dev, :] = xin[patch, video].astype(jnp.float32)
    mixed = norm_tokens(xf[...], par_ref[0])
    for step in range(count - 1):
        ring_step(0, step)
        if step == count - 3:
            ring_start(1)
    own_w.wait()
    sibling_done(0)
    query, key, value = project(0, mixed)
    ring_step(1, 0)
    attended = attend_heads(
        query, key, value, heads_map, mask_ref[0], att, head_size, lambda: ring_step(1, 1)
    )
    ring_step(1, 2)
    xf[...] = update(0, xf[...], attended)

    frame = core * count + me
    for k in range(2 * count):
        video, patch = k // count, k % count
        low = k * patch_dev
        mid_send[k] = xf[low : low + patch_dev, :].astype(jnp.bfloat16)
    own_mid = pltpu.make_async_copy(mid_send.at[frame], mid_recv.at[frame], local_sem.at[2])
    own_mid.start()
    for s in range(2):
        for k in range(count):
            if k or s:
                peer, video = lax.rem(me + k, count), lax.rem(core + s, 2)
                copy = remote(
                    mid_send.at[video * count + peer],
                    mid_recv.at[frame],
                    mid_ssem.at[s * count + k],
                    mid_rsem.at[frame],
                    peer,
                    video,
                )
                copy.start()
                sent.append(copy)
    for step in range(3, count - 1):
        ring_step(1, step)
    own_mid.wait()
    for s in range(2):
        for k in range(count):
            if k or s:
                peer, video = lax.rem(me + k, count), lax.rem(core + s, 2)
                landed = mid_recv.at[video * count + peer]
                remote(
                    landed,
                    landed,
                    mid_ssem.at[s * count + k],
                    mid_rsem.at[video * count + peer],
                    peer,
                    video,
                ).wait_recv()

    for k in range(2 * count):
        low = k * patch_dev
        xf[low : low + patch_dev, :] = mid_recv[k].astype(jnp.float32)
    mixed = norm_tokens(xf[...], par_ref[1])
    sibling_done(1)
    query, key, value = project(1, mixed)
    attended = attend_heads(query, key, value, heads_map, mask_ref[1], att, head_size)
    xf[...] = update(1, xf[...], attended)
    for k in range(2 * count):
        low = k * patch_dev
        res[k] = xf[low : low + patch_dev, :].astype(jnp.bfloat16)
    own_out = pltpu.make_async_copy(
        res.at[pl.ds(core * count, count)], out_ref.at[core], local_sem.at[3]
    )
    own_out.start()
    final = remote(
        res.at[pl.ds(sib * count, count)], out_ref.at[core], fin_send, fin_recv, me, sib
    )
    final.start()
    own_out.wait()
    final.wait_send()
    remote(
        out_ref.at[sib], out_ref.at[sib], fin_send, fin_recv, me, sib
    ).wait_recv()
    for copy in sent:
        copy.wait_send()


def fused_device(video_tokens, timestep, w_qkv, w_out, qk_gain, mod_table, mod_gain):
    videos, fr_dev, patch_dev, width = video_tokens.shape
    layers, rows, _ = w_qkv.shape
    head_size = qk_gain.shape[2]
    feat = w_out.shape[1]
    heads = feat // head_size
    tokens = videos * fr_dev * patch_dev
    embed = time_embed(timestep, width)
    params = mod_table + mod_gain * embed[None, None, :]
    gains = jnp.tile(qk_gain, (1, 1, heads))
    joined = jnp.concatenate([w_qkv, w_out.transpose(0, 2, 1)], axis=2)
    lanes = joined.shape[2]
    heads_map = jnp.asarray(np.repeat(np.eye(heads, dtype=np.float32), head_size, axis=1))
    row = np.arange(tokens)
    frame_patches = tokens // videos
    masks = np.stack(
        [
            (row[:, None] // frame_patches) == (row[None, :] // frame_patches),
            (row[:, None] % patch_dev) == (row[None, :] % patch_dev),
        ]
    ).astype(np.float32)
    vmem = pl.BlockSpec(memory_space=pltpu.VMEM)
    count = fr_dev
    bf16, f32 = jnp.bfloat16, jnp.float32
    dma = pltpu.SemaphoreType.DMA
    ring = (layers, count - 1, CHUNKS)
    return pl.pallas_call(
        functools.partial(fused_kernel, head_size),
        out_shape=jax.ShapeDtypeStruct(video_tokens.shape, bf16),
        in_specs=[pl.BlockSpec(memory_space=pl.ANY)] + [vmem] * 5,
        out_specs=vmem,
        scratch_shapes=[
            pltpu.VMEM((layers, count * rows, lanes), bf16),
            pltpu.VMEM((count, videos, patch_dev, width), bf16),
            pltpu.VMEM((2 * count, patch_dev, width), bf16),
            pltpu.VMEM((2 * count, patch_dev, width), bf16),
            pltpu.VMEM((tokens, width), f32),
            pltpu.VMEM((tokens, feat), f32),
            pltpu.VMEM((2 * count, patch_dev, width), bf16),
            dma((4,)),
            dma((count,)),
            dma((count,)),
            dma(ring[:2] + (2,)),
            dma(ring[:2] + (2,)),
            dma(ring),
            dma(ring),
            dma((2 * count,)),
            dma((2 * count,)),
            dma,
            dma,
            dma((layers, count - 1)),
            dma((layers, count - 1)),
        ],
        compiler_params=pltpu.CompilerParams(
            collective_id=0, has_side_effects=True, vmem_limit_bytes=56 * 1024 * 1024
        ),
        name="blocks",
    )(video_tokens, joined, params, gains, heads_map, jnp.asarray(masks))


def choose_device(video_tokens, timestep, w_qkv, *rest):
    videos, fr_dev, _, _ = video_tokens.shape
    fits = videos == 2 and fr_dev == 8 and w_qkv.shape[1] % (16 * CHUNKS) == 0
    run = fused_device if fits else per_device
    return run(video_tokens, timestep, w_qkv, *rest)


def solution(mesh):
    placed = (
        P("grp", "frame", "patch", None),
        P("grp"),
        P(None, "patch", None),
        P(None, None, "patch"),
        P(),
        P(),
        P(),
    )
    ring = (mesh.shape["grp"], mesh.shape["patch"], mesh.shape["frame"]) == (2, 8, 2)
    return jax.shard_map(
        choose_device if ring else per_device,
        mesh=mesh,
        in_specs=placed,
        out_specs=P("grp", "frame", "patch", None),
        check_vma=False,
    )
```
